32 devices in a mesh: row: 16 (over z, y, x), col: 2 (over core).
Axes of the slice: x: 2, y: 2, z: 4, core: 2. Of those that a mesh axis runs over, the one named last changes fastest.
Arguments:
- image_embeddings: bfloat16 [128, 64, 1024], P('row', 'col'), may hold values from -6 to 6
- lagged_blend_ratios: float32 [3, 1024], replicated, may hold values from 0.05 to 0.95
- linear_map_coefficients: bfloat16 [3, 1024, 1024], P(None, 'row'), may hold values from -0.1875 to 0.1875
- retention_exponent: float32 [16, 128, 64], P(None, 'row', 'col'), may hold values from -3 to 0, as said below
- self_credit: float32 [1024], replicated, may hold values from 1 to 8
- channel_scale_vector: float32 [1024], replicated, may hold values from 0.5 to 2
- pooling_scale_vector: float32 [4096], replicated, may hold values from 0.5 to 2
- pooling_offset_vector: float32 [4096], replicated, may hold values from -3 to 3
Outputs:
- merged: bfloat16 [64, 32, 4096], P('row', 'col')
The draws below stay inside these ranges and needn't reach their ends.
Inputs may be any that keep to these rules, and one draw needn't show every extreme that they name: `retention_exponent`: the logarithm of the share of a head's state kept at each patch.
All inputs are finite; a program needn't handle non-finite values.
Results may differ from the reference program's by a relative error of at most 0.0057.
Values may be sent and summed in bfloat16 or wider, within the bound.
A program may use at most 192 MiB of HBM per device.

```python
import math
import jax
import jax.numpy as jnp
from jax import lax

EMBEDDING_SIZE = 1024
HEAD_COUNT = 16
HEAD = 64
R_DEV = 8
STRIP_COLUMNS = 32
PATCH_ROWS = 128
PATCH_COLUMNS = 64
N_ROW = 16
N_COL = 2


def draw_retention_exponent(key, part):
    direction_flows = jax.random.split(jax.random.fold_in(key, 11), 9)
    chain_length = PATCH_ROWS * STRIP_COLUMNS
    block_length = R_DEV * STRIP_COLUMNS
    row_blocks = PATCH_ROWS // R_DEV
    column_block_count = PATCH_COLUMNS // STRIP_COLUMNS
    fast_heads = max(1, HEAD_COUNT * 3 // 16)
    middle_heads = max(1, HEAD_COUNT * 5 // 16)
    ranking = jax.random.permutation(direction_flows[0], HEAD_COUNT)
    is_fast = ranking < fast_heads
    is_middle = (ranking >= fast_heads) & (ranking < fast_heads + middle_heads)
    fast_rate = 2.3 / 40.0 * jnp.exp(jax.random.uniform(direction_flows[1], (HEAD_COUNT,), minval=-0.3, maxval=0.3))
    slow_rate = 0.35 / chain_length * jnp.exp(jax.random.uniform(direction_flows[2], (HEAD_COUNT,), minval=-0.7, maxval=0.7))
    middle_rate = 1.0 / block_length * jnp.exp(jax.random.uniform(direction_flows[8], (HEAD_COUNT,), minval=-0.5, maxval=0.5))
    base_rate = jnp.where(is_fast, fast_rate, jnp.where(is_middle, middle_rate, slow_rate))
    token_factor = jnp.exp(jax.random.uniform(direction_flows[3], (HEAD_COUNT, PATCH_ROWS, PATCH_COLUMNS), minval=-0.7, maxval=0.7))
    block_factor = jnp.exp(jax.random.uniform(direction_flows[4], (HEAD_COUNT, row_blocks, 1, column_block_count, 1), minval=-0.7, maxval=0.7))
    block_factor = jnp.broadcast_to(block_factor, (HEAD_COUNT, row_blocks, R_DEV, column_block_count, STRIP_COLUMNS)).reshape(HEAD_COUNT, PATCH_ROWS, PATCH_COLUMNS)
    decay_rates = -base_rate[:, None, None] * token_factor * block_factor
    span_rows = jax.random.randint(direction_flows[5], (3, HEAD_COUNT, 1, column_block_count, 1), 0, PATCH_ROWS)
    span_columns = jax.random.randint(direction_flows[6], (3, HEAD_COUNT, 1, column_block_count, 1), 0, STRIP_COLUMNS)
    span_length = jnp.log(jax.random.uniform(direction_flows[7], (3, HEAD_COUNT, 1, column_block_count, 1), minval=0.5, maxval=0.8))
    row_position = jnp.arange(PATCH_ROWS).reshape(1, PATCH_ROWS, 1, 1)
    column_position = jnp.arange(STRIP_COLUMNS).reshape(1, 1, 1, STRIP_COLUMNS)
    for group_span in range(3):
        matched_mask = (row_position == span_rows[group_span]) & (column_position == span_columns[group_span])
        decay_rates = decay_rates + jnp.where(matched_mask, span_length[group_span], 0.0).reshape(HEAD_COUNT, PATCH_ROWS, PATCH_COLUMNS)
    return decay_rates.astype(jnp.float32)


def block_levels(rng, shape, pieces, least, high):
    def one(dim, parts):
        heights = jax.random.uniform(jax.random.fold_in(jax.random.fold_in(rng, 6), dim), (parts,), jnp.float32, least / len(pieces), high / len(pieces))
        return jnp.repeat(jnp.exp(heights), shape[dim] // parts).reshape((-1,) + (1,) * (len(shape) - dim - 1))

    factor_of = one(*pieces[0])
    for cut in pieces[1:]:
        factor_of = factor_of * one(*cut)
    return factor_of


def bell_draw(key, dims, scale, reach, pieces=(), kind=jnp.bfloat16):
    entries = scale * jax.random.normal(key, dims, jnp.float32)
    if pieces:
        entries = entries * block_levels(key, dims, pieces, -0.22, 0.18)
    return jnp.clip(entries, -reach, reach).astype(kind)


def setup_inputs(seed: int = 0) -> dict:
    streams_of = jax.random.split(jax.random.key(seed), 9)
    return {
        "image_embeddings": bell_draw(streams_of[0], (PATCH_ROWS, PATCH_COLUMNS, EMBEDDING_SIZE), 1.0, 6.0, ((0, 16), (1, 2))),
        "lagged_blend_ratios": jnp.clip(jax.random.uniform(streams_of[1], (3, EMBEDDING_SIZE), jnp.float32, 0.05, 0.95), 0.05, 0.95),
        "linear_map_coefficients": bell_draw(streams_of[2], (3, EMBEDDING_SIZE, EMBEDDING_SIZE), EMBEDDING_SIZE ** -0.5, 0.1875, ((1, 16),)),
        "retention_exponent": draw_retention_exponent(jax.random.fold_in(streams_of[8], 71), 0),
        "self_credit": jnp.clip(jnp.exp(jax.random.uniform(streams_of[4], (EMBEDDING_SIZE,), jnp.float32, math.log(1.0), math.log(8.0))), 1.0, 8.0),
        "channel_scale_vector": jnp.clip(jnp.exp(jax.random.uniform(streams_of[5], (EMBEDDING_SIZE,), jnp.float32, math.log(0.5), math.log(2.0))), 0.5, 2.0),
        "pooling_scale_vector": jnp.clip(jnp.exp(jax.random.uniform(streams_of[6], (4 * EMBEDDING_SIZE,), jnp.float32, math.log(0.5), math.log(2.0))), 0.5, 2.0),
        "pooling_offset_vector": bell_draw(streams_of[7], (4 * EMBEDDING_SIZE,), 0.5, 3.0, (), jnp.float32),
    }


PRECISE = lax.Precision.HIGHEST

def head_mix(argument_tensors):
    query_head, key_head, value_head, running, before = argument_tensors
    count = query_head.shape[0]
    position = jnp.arange(count, dtype=jnp.int32)
    earlier_mask = position[:, None] > position[None, :]
    diagonal = position[:, None] == position[None, :]
    scores = jnp.dot(query_head, key_head.T, preferred_element_type=jnp.float32)
    exponent = jnp.where(earlier_mask, before[:, None] - running[None, :], before[None, :] - running[:, None])
    weights = jnp.where(diagonal, jnp.float32(0.0), jnp.exp(exponent))
    pair_weight = (scores * weights).astype(jnp.bfloat16)
    return jnp.dot(pair_weight, value_head, preferred_element_type=jnp.float32)

def block_states(argument_tensors):
    address_vectors, content_vectors, retention_ratio = argument_tensors
    count, width = address_vectors.shape
    attention_units = retention_ratio.shape[0]
    unit_dimension = width // attention_units
    running = jnp.cumsum(retention_ratio, axis=1)
    before = running - retention_ratio
    total = running[:, -1:]
    unitwise_addresses = address_vectors.astype(jnp.float32).reshape(count, attention_units, unit_dimension)
    unitwise_contents = content_vectors.astype(jnp.float32).reshape(count, attention_units, unit_dimension)
    forward_state = jnp.einsum('thd,the->hde', unitwise_addresses * jnp.exp(total - running).T[:, :, None], unitwise_contents, precision=PRECISE)
    backward_state = jnp.einsum('thd,the->hde', unitwise_addresses * jnp.exp(before).T[:, :, None], unitwise_contents, precision=PRECISE)
    return (jnp.exp(total[:, 0]), forward_state, backward_state)

def segment_routine(argument_tensors):
    content_vectors_full, acceptance_vectors, address_vectors, content_vectors, retention_ratio, ordered_sequence, reversed_sequence, self_credit, channel_scale_vector = argument_tensors
    count, width = acceptance_vectors.shape
    attention_units = retention_ratio.shape[0]
    unit_dimension = width // attention_units
    running = jnp.cumsum(retention_ratio, axis=1)
    before = running - retention_ratio
    total = running[:, -1:]

    def per_head(matrix):
        return matrix.reshape(count, attention_units, unit_dimension).transpose(1, 0, 2)
    local = lax.map(head_mix, (per_head(acceptance_vectors), per_head(address_vectors), per_head(content_vectors), running, before))
    unitwise_probes = acceptance_vectors.astype(jnp.float32).reshape(count, attention_units, unit_dimension)
    unitwise_addresses = address_vectors.astype(jnp.float32).reshape(count, attention_units, unit_dimension)
    unitwise_contents = content_vectors.astype(jnp.float32).reshape(count, attention_units, unit_dimension)
    carried = jnp.exp(before).T[:, :, None] * jnp.einsum('thd,hde->the', unitwise_probes, ordered_sequence, precision=PRECISE)
    carried = carried + jnp.exp(total - running).T[:, :, None] * jnp.einsum('thd,hde->the', unitwise_probes, reversed_sequence, precision=PRECISE)
    principal_summand = lax.optimization_barrier(jnp.sum(unitwise_probes * self_credit.reshape(attention_units, unit_dimension) * unitwise_addresses, axis=2, keepdims=True)) * unitwise_contents
    wkv_out = local.transpose(1, 0, 2) + carried + principal_summand
    centred = wkv_out - lax.optimization_barrier(jnp.mean(wkv_out, axis=2, keepdims=True))
    variance = lax.optimization_barrier(jnp.mean(centred * centred, axis=2, keepdims=True))
    normed = centred * lax.rsqrt(variance + 1e-05) * channel_scale_vector.reshape(attention_units, unit_dimension)
    return (content_vectors_full.reshape(count, attention_units, unit_dimension) + normed).reshape(count, width)

def merge_tiles(block_out, pooling_scale_vector, pooling_offset_vector):
    tile_rows, tile_cols, width = block_out.shape
    grouped = block_out.reshape(tile_rows // 2, 2, tile_cols // 2, 2, width).transpose(0, 2, 3, 1, 4)
    grouped = grouped.reshape(tile_rows // 2, tile_cols // 2, 4 * width)
    merge_centred = grouped - lax.optimization_barrier(jnp.mean(grouped, axis=2, keepdims=True))
    variance = lax.optimization_barrier(jnp.mean(merge_centred * merge_centred, axis=2, keepdims=True))
    return (merge_centred * lax.rsqrt(variance + 1e-05) * pooling_scale_vector + pooling_offset_vector).astype(jnp.bfloat16)

def reference(image_embeddings, lagged_blend_ratios, linear_map_coefficients, retention_exponent, self_credit, channel_scale_vector, pooling_scale_vector, pooling_offset_vector):
    quarter = EMBEDDING_SIZE // 4
    quadrant_piece = R_DEV * STRIP_COLUMNS
    padded = jnp.pad(image_embeddings, ((1, 1), (1, 1), (0, 0)))

    def one_strip(strip):
        first = (strip * STRIP_COLUMNS).astype(jnp.int32)
        window = lax.dynamic_slice_in_dim(padded, first, STRIP_COLUMNS + 2, 1)
        centre = window[1:-1, 1:-1]
        shifted = jnp.concatenate([window[1:-1, :-2, :quarter], window[1:-1, 2:, quarter:2 * quarter], window[:-2, 1:-1, 2 * quarter:3 * quarter], window[2:, 1:-1, 3 * quarter:]], axis=2)
        content_vectors_full = centre.astype(jnp.float32)
        shifted_float = shifted.astype(jnp.float32)
        mapped_embeddings = []
        for index in range(3):
            mixed = (content_vectors_full * lagged_blend_ratios[index] + shifted_float * (1.0 - lagged_blend_ratios[index])).astype(jnp.bfloat16)
            product = jnp.dot(mixed.reshape(PATCH_ROWS * STRIP_COLUMNS, EMBEDDING_SIZE), linear_map_coefficients[index], preferred_element_type=jnp.float32)
            mapped_embeddings.append(product.astype(jnp.bfloat16).reshape(N_ROW, quadrant_piece, EMBEDDING_SIZE))
        retention_ratio = lax.dynamic_slice_in_dim(retention_exponent, first, STRIP_COLUMNS, 2).reshape(HEAD_COUNT, N_ROW, quadrant_piece).transpose(1, 0, 2)
        kept, forward_state, backward_state = lax.map(block_states, (mapped_embeddings[1], mapped_embeddings[2], retention_ratio))

        def carry_step(state, item):
            return (item[0][:, None, None] * state + item[1], state)
        start_state = jnp.zeros((HEAD_COUNT, HEAD, HEAD), jnp.float32)
        ordered_sequence = lax.scan(carry_step, start_state, (kept, forward_state))[1]
        reversed_sequence = lax.scan(carry_step, start_state, (kept, backward_state), reverse=True)[1]
        self_credit_table = jnp.broadcast_to(self_credit, (N_ROW, EMBEDDING_SIZE))
        scaling_table = jnp.broadcast_to(channel_scale_vector, (N_ROW, EMBEDDING_SIZE))
        result_tensors = lax.map(segment_routine, (content_vectors_full.reshape(N_ROW, quadrant_piece, EMBEDDING_SIZE), mapped_embeddings[0], mapped_embeddings[1], mapped_embeddings[2], retention_ratio, ordered_sequence, reversed_sequence, self_credit_table, scaling_table))
        return merge_tiles(result_tensors.reshape(PATCH_ROWS, STRIP_COLUMNS, EMBEDDING_SIZE), pooling_scale_vector, pooling_offset_vector)
    merged = lax.map(one_strip, jnp.arange(N_COL, dtype=jnp.int32))
    return merged.transpose(1, 0, 2, 3).reshape(PATCH_ROWS // 2, PATCH_COLUMNS // 2, 4 * EMBEDDING_SIZE)
```

```python
import functools

import jax
import jax.numpy as jnp
from jax import lax
from jax.experimental import pallas as pl
from jax.experimental.pallas import tpu as pltpu
from jax.sharding import PartitionSpec as P

MESH = pl.DeviceIdType.MESH
F32 = jnp.float32
BF16 = jnp.bfloat16
HIGH = lax.Precision.HIGHEST
UP, DOWN, FIRST, SECOND, MATE = range(5)


def iota(shape, dim):
    return lax.broadcasted_iota(jnp.int32, shape, dim)


def kernel(
    rows, cols, tile_rows, tile_cols, heads,
    x_ref, ratio_ref, w_ref, ret_ref, credit_ref, gain_ref, scale_ref, offset_ref,
    out_ref,
    wf, mx, proj, decay, halo_side, halo_row, run_c, mine, totals, states, arrived, scan_f, leaving,
    entering, block, stats,
    w_send, w_recv, halo_send, halo_recv, t_send, t_recv, a_send, a_recv, b_send, b_recv,
):
    count, width = x_ref.shape
    hd = width // heads
    pairs = heads // 2
    lanes = 2 * hd
    quarter = width // 4
    share = w_ref.shape[1]
    half_w = width // 2
    unit = states.shape[1]
    row, col = lax.axis_index("row"), lax.axis_index("col")
    plane = 4
    depth = rows // plane
    z, q = row // plane, row % plane
    bx, by = q % 2, q // 2
    half = col % 2
    mate = col + 1 - 2 * half
    q1 = (1 - half) * (q + 1 - 2 * bx) + half * (q + 2 - 4 * by)
    q2 = half * (q + 1 - 2 * bx) + (1 - half) * (q + 2 - 4 * by)
    q12 = plane - 1 - q

    barrier = pltpu.get_barrier_semaphore()

    def greet(o, carry):
        pl.semaphore_signal(barrier, inc=1, device_id={"row": (row + o) % rows}, device_id_type=MESH)
        return carry

    lax.fori_loop(1, rows, greet, 0)
    right, left = (col + 1) % cols, (col + cols - 1) % cols
    for other in (right, left, mate):
        pl.semaphore_signal(barrier, inc=1, device_id={"col": other}, device_id_type=MESH)
    pl.semaphore_wait(barrier, rows + 2)

    down_row, up_row = (row + 1) % rows, (row + rows - 1) % rows
    halos = [
        pltpu.make_async_remote_copy(
            x_ref.at[:, 0:quarter], halo_side.at[0], halo_send.at[0], halo_recv.at[0],
            device_id={"col": right}, device_id_type=MESH),
        pltpu.make_async_remote_copy(
            x_ref.at[:, quarter:2 * quarter], halo_side.at[1], halo_send.at[1], halo_recv.at[1],
            device_id={"col": left}, device_id_type=MESH),
        pltpu.make_async_remote_copy(
            x_ref.at[count - tile_cols:count, 2 * quarter:3 * quarter], halo_row.at[0],
            halo_send.at[2], halo_recv.at[2], device_id={"row": down_row}, device_id_type=MESH),
        pltpu.make_async_remote_copy(
            x_ref.at[0:tile_cols, 3 * quarter:], halo_row.at[1],
            halo_send.at[3], halo_recv.at[3], device_id={"row": up_row}, device_id_type=MESH),
    ]
    for h in halos:
        h.start()

    def sl(g):
        return pl.ds(1, 2) if g == 0 else pl.ds(0, 1)

    def place(g, side, src):
        return wf.at[sl(g), side, pl.ds(pl.multiple_of(src * share, share), share), :]

    targets = {
        UP: {"row": (row + plane) % rows},
        DOWN: {"row": (row + rows - plane) % rows},
        FIRST: {"row": z * plane + q1},
        SECOND: {"row": z * plane + q2},
        MATE: {"col": mate},
    }

    def send(g, kind, src, own=False):
        source = place(g, half, src)
        if own:
            source = w_ref.at[sl(g), :, pl.ds(pl.multiple_of(half * half_w, half_w), half_w)]
        return pltpu.make_async_remote_copy(
            source, place(g, half, src), w_send.at[g, kind, src], w_recv.at[g, half, src],
            device_id=targets[kind], device_id_type=MESH)

    def got(g, side, src):
        ref = place(g, side, src)
        pltpu.make_async_remote_copy(
            ref, ref, w_send.at[g, MATE, src], w_recv.at[g, side, src],
            device_id=targets[MATE], device_id_type=MESH).wait_recv()

    can_up, can_down = z < depth - 1, z > 0

    def own_step(g):
        @pl.when(can_up)
        def _():
            send(g, UP, row, True).start()

        @pl.when(can_down)
        def _():
            send(g, DOWN, row, True).start()

        send(g, SECOND, row, True).start()
        send(g, FIRST, row, True).start()

    def both(d, act):
        if d == 0:
            act(z, None)
            return

        @pl.when(z >= d)
        def _():
            act(z - d, UP)

        @pl.when(z + d < depth)
        def _():
            act(z + d, DOWN)

    def z_step(g, d):
        def act(zz, onward):
            src = zz * plane + q
            got(g, half, src)

            @pl.when(can_up if onward == UP else can_down)
            def _():
                send(g, onward, src).start()

            for kind in (SECOND, FIRST, MATE):
                send(g, kind, src).start()

        both(d, act)

    def first_step(g, d):
        def act(zz, onward):
            src = zz * plane + q1
            got(g, half, src)
            send(g, SECOND, src).start()
            send(g, MATE, src).start()

        both(d, act)

    def second_step(g, d):
        def act(zz, onward):
            for qq in (q2, q12):
                src = zz * plane + qq
                got(g, half, src)
                send(g, MATE, src).start()

        both(d, act)

    def mate_wait(g):
        def one(o, carry):
            got(g, 1 - half, (row + o) % rows)
            return carry

        lax.fori_loop(1, rows, one, 0)

    own_step(0)

    at = pl.ds(pl.multiple_of(row * share, share), share)
    for p in range(3):
        for side in range(2):
            wf[p, side, at, :] = w_ref[p, :, side * half_w:(side + 1) * half_w]

    ret = ret_ref[...]
    tri = (iota((count, count), 0) >= iota((count, count), 1)).astype(F32)
    running_c = lax.dot_general(tri, ret, (((1,), (1,)), ((), ())), precision=HIGH, preferred_element_type=F32)
    running_r = lax.dot_general(ret, tri, (((1,), (1,)), ((), ())), precision=HIGH, preferred_element_type=F32)
    eye = (iota((count, count), 0) == iota((count, count), 1)).astype(F32)
    ret_c = lax.dot_general(eye, ret, (((1,), (1,)), ((), ())), precision=HIGH, preferred_element_type=F32)
    before_c = running_c - ret_c
    before_r = running_r - ret
    total_r = running_c[count - 1:count, :]
    run_c[0] = running_c
    run_c[1] = before_c
    run_c[2] = total_r - running_c
    mine[...] = jnp.broadcast_to(
        jnp.concatenate([total_r, jnp.zeros((1, 128 - heads), F32)], axis=1), (8, 128))
    totals[row] = mine[...]

    def picked(table, h):
        return jnp.sum(jnp.where(iota(table.shape, 1) == h, table, 0.0), axis=1, keepdims=True)

    def picked_row(table, h):
        return jnp.sum(jnp.where(iota(table.shape, 0) == h, table, 0.0), axis=0, keepdims=True)

    def total_copy(o):
        to = (row + o) % rows
        return pltpu.make_async_remote_copy(
            mine, totals.at[row], t_send.at[to], t_recv.at[row],
            device_id={"row": to}, device_id_type=MESH)

    def total_send(o, carry):
        total_copy(o).start()
        return carry

    lax.fori_loop(1, rows, total_send, 0)

    z_step(0, 1) if depth > 1 else None
    first_step(0, 0)
    second_step(0, 0)

    for h in halos:
        h.wait()
    token = iota((count, quarter), 0)
    place_in_row = token % tile_cols
    x0 = x_ref[:, 0:quarter].astype(F32)
    x1 = x_ref[:, quarter:2 * quarter].astype(F32)
    side0 = jnp.where(col > 0, halo_side[0].astype(F32), 0.0)
    side1 = jnp.where(col < cols - 1, halo_side[1].astype(F32), 0.0)
    top = jnp.where(row > 0, halo_row[0].astype(F32), 0.0)
    bottom = jnp.where(row < rows - 1, halo_row[1].astype(F32), 0.0)
    last = tile_cols - 1
    shifted = [
        jnp.where(place_in_row == 0, pltpu.roll(side0, count - last, 0), pltpu.roll(x0, 1, 0)),
        jnp.where(place_in_row == last, pltpu.roll(side1, last, 0), pltpu.roll(x1, count - 1, 0)),
        jnp.concatenate([top, x_ref[0:count - tile_cols, 2 * quarter:3 * quarter].astype(F32)], axis=0),
        jnp.concatenate([x_ref[tile_cols:count, 3 * quarter:].astype(F32), bottom], axis=0),
    ]
    for part in range(4):
        span = slice(part * quarter, (part + 1) * quarter)
        xs = x_ref[:, span].astype(F32)
        for p in range(3):
            c = ratio_ref[p:p + 1, span]
            mx[p, :, span] = (xs * c + shifted[part] * (1.0 - c)).astype(BF16)

    for d in range(2, depth):
        z_step(0, d)
        first_step(0, d - 1)
        second_step(0, d - 1)
    if depth > 1:
        first_step(0, depth - 1)
        second_step(0, depth - 1)
    own_step(1)

    earlier = iota((count, count), 0) > iota((count, count), 1)
    diagonal = iota((count, count), 0) == iota((count, count), 1)

    def decays(h, carry):
        rc, bc = picked(run_c[0], h), picked(run_c[1], h)
        rr, br = picked_row(running_r, h), picked_row(before_r, h)
        exponent = jnp.where(earlier, bc - rr, br - rc)
        decay[h] = jnp.where(diagonal, 0.0, jnp.exp(exponent))
        return carry

    lax.fori_loop(0, heads, decays, 0)

    mate_wait(0)

    def project(p):
        for side in range(2):
            def chunk(i, carry):
                src = pl.ds(pl.multiple_of(i * 256, 256), 256)
                dst = pl.ds(pl.multiple_of(side * half_w + i * 256, 256), 256)
                proj[p, :, dst] = jnp.dot(
                    mx[p], wf[p, side, :, src], preferred_element_type=F32).astype(BF16)
                return carry

            lax.fori_loop(0, half_w // 256, chunk, 0)

    project(1)
    project(2)

    lane = iota((count, lanes), 1)
    low = lane < hd

    def pair_col(table, i):
        return jnp.where(low, picked(table, 2 * i), picked(table, 2 * i + 1))

    low_u = iota((hd, lanes), 1) < hd
    flat = rows * unit

    def local_states(i, carry):
        span = pl.ds(pl.multiple_of(i * lanes, lanes), lanes)
        k = proj[1, :, span].astype(F32)
        v = proj[2, :, span]
        kd = jnp.concatenate(
            [k * jnp.exp(pair_col(run_c[2], i)), k * jnp.exp(pair_col(run_c[1], i))], axis=1).astype(BF16)
        m = lax.dot_general(kd, v, (((0,), (0,)), ((), ())), preferred_element_type=F32)
        a = jnp.where(low_u, m[0:hd], pltpu.roll(m[2 * hd:3 * hd], hd, 1)).astype(BF16)
        b = jnp.where(low_u, pltpu.roll(m[hd:2 * hd], hd, 1), m[3 * hd:]).astype(BF16)
        per = hd // unit
        for s in range(per):
            states[2 * i * per + s] = a[s * unit:(s + 1) * unit]
            states[(2 * i + 1) * per + s] = b[s * unit:(s + 1) * unit]
        return carry

    lax.fori_loop(0, pairs, local_states, 0)

    def a_copy(o):
        to = (row + o) % rows
        return pltpu.make_async_remote_copy(
            states.at[to], arrived.at[row], a_send.at[to], a_recv.at[row],
            device_id={"row": to}, device_id_type=MESH)

    def a_start(o, carry):
        a_copy(o).start()
        return carry

    lax.fori_loop(1, rows, a_start, 0)
    arrived[row] = states[row]

    z_step(1, 1) if depth > 1 else None
    first_step(1, 0)
    second_step(1, 0)
    if depth > 2:
        z_step(1, 2)
        first_step(1, 1)
        second_step(1, 1)

    def from_all(dst, send_sem, recv_sem):
        def one(o, carry):
            src = (row + o) % rows
            pltpu.make_async_remote_copy(
                dst.at[src], dst.at[src], send_sem.at[src], recv_sem.at[src],
                device_id={"row": src}, device_id_type=MESH).wait_recv()
            return carry

        lax.fori_loop(1, rows, one, 0)

    from_all(totals, t_send, t_recv)
    from_all(arrived, a_send, a_recv)
    head = (row * unit) // hd

    def kept(j):
        return jnp.exp(picked(totals[j], head))[0:1, :]

    def forward(j, acc):
        scan_f[j] = acc
        return kept(j) * acc + arrived[j].astype(F32)

    def backward(o, acc):
        j = rows - 1 - o
        leaving[j] = jnp.where(iota((unit, lanes), 1) < hd, scan_f[j], acc).astype(BF16)
        return kept(j) * acc + arrived[j].astype(F32)

    lax.fori_loop(0, rows, forward, jnp.zeros((unit, lanes), F32))
    lax.fori_loop(0, rows, backward, jnp.zeros((unit, lanes), F32))

    def b_copy(o):
        to = (row + o) % rows
        return pltpu.make_async_remote_copy(
            leaving.at[to], entering.at[row], b_send.at[to], b_recv.at[row],
            device_id={"row": to}, device_id_type=MESH)

    def b_start(o, carry):
        b_copy(o).start()
        return carry

    lax.fori_loop(1, rows, b_start, 0)
    entering[row] = leaving[row]

    for d in range(3, depth):
        z_step(1, d)
        first_step(1, d - 1)
        second_step(1, d - 1)
    if depth > 1:
        first_step(1, depth - 1)
        second_step(1, depth - 1)
    mate_wait(1)
    project(0)

    def halves(value):
        a = jnp.sum(jnp.where(low, value, 0.0), axis=1, keepdims=True)
        b = jnp.sum(jnp.where(low, 0.0, value), axis=1, keepdims=True)
        return jnp.where(low, a, b)

    def local_mix(i, carry):
        span = pl.ds(pl.multiple_of(i * lanes, lanes), lanes)
        r, k, v = proj[0, :, span], proj[1, :, span], proj[2, :, span]
        outs = []
        for s in range(2):
            rs = jnp.where(low if s == 0 else jnp.logical_not(low), r.astype(F32), 0.0).astype(BF16)
            scores = lax.dot_general(rs, k, (((1,), (1,)), ((), ())), preferred_element_type=F32)
            weight = (scores * decay[2 * i + s]).astype(BF16)
            outs.append(jnp.dot(weight, v, preferred_element_type=F32))
        own = halves(r.astype(F32) * credit_ref[:, span] * k.astype(F32)) * v.astype(F32)
        block[i] = jnp.where(low, outs[0], outs[1]) + own
        return carry

    lax.fori_loop(0, pairs, local_mix, 0)
    from_all(entering, b_send, b_recv)

    def finish(i, total):
        span = pl.ds(pl.multiple_of(i * lanes, lanes), lanes)
        r = proj[0, :, span]
        per = hd // unit
        a = jnp.concatenate([entering[2 * i * per + s].astype(F32) for s in range(per)], axis=0)
        b = jnp.concatenate([entering[(2 * i + 1) * per + s].astype(F32) for s in range(per)], axis=0)
        fwd = jnp.concatenate(
            [jnp.where(low_u, a, 0.0), jnp.where(low_u, 0.0, pltpu.roll(b, hd, 1))], axis=0).astype(BF16)
        bwd = jnp.concatenate(
            [jnp.where(low_u, pltpu.roll(a, hd, 1), 0.0), jnp.where(low_u, 0.0, b)], axis=0).astype(BF16)
        wkv = (
            block[i]
            + jnp.exp(pair_col(run_c[1], i)) * jnp.dot(r, fwd, preferred_element_type=F32)
            + jnp.exp(pair_col(run_c[2], i)) * jnp.dot(r, bwd, preferred_element_type=F32)
        )
        centred = wkv - halves(wkv) * (1.0 / hd)
        variance = halves(centred * centred) * (1.0 / hd)
        made = x_ref[:, span].astype(F32) + centred * lax.rsqrt(variance + 1e-05) * gain_ref[:, span]
        block[i] = made
        return total + made

    total = lax.fori_loop(0, pairs, finish, jnp.zeros((count, lanes), F32))
    group = (
        (iota((count, count), 0) // (2 * tile_cols) == iota((count, count), 1) // (2 * tile_cols))
        & (iota((count, count), 0) % tile_cols // 2 == iota((count, count), 1) % tile_cols // 2)
    ).astype(F32)

    def over_group(value):
        rowsum = jnp.broadcast_to(jnp.sum(value, axis=1, keepdims=True), (count, lanes))
        return jnp.dot(group, rowsum, precision=HIGH, preferred_element_type=F32) * (1.0 / (4 * width))

    mean = over_group(total)

    def spread(i, acc):
        dev = block[i] - mean
        return acc + dev * dev

    variance = over_group(lax.fori_loop(0, pairs, spread, jnp.zeros((count, lanes), F32)))
    stats[0] = mean
    stats[1] = lax.rsqrt(variance + 1e-05)
    half_cols = tile_cols // 2

    def emit(i, carry):
        for part in range(4):
            span = pl.ds(pl.multiple_of(part * width + i * lanes, lanes), lanes)
            g, o = scale_ref[:, span], offset_ref[:, span]
            for a in range(tile_rows // 2):
                take = pl.ds((2 * a + part % 2) * tile_cols + part // 2, half_cols, stride=2)
                value = (block[i, take, :] - stats[0, take, :]) * stats[1, take, :]
                out_ref[a, :, span] = (value * g + o).astype(BF16)
        return carry

    lax.fori_loop(0, pairs, emit, 0)

    def drain(o, carry):
        total_copy(o).wait_send()
        a_copy(o).wait_send()
        b_copy(o).wait_send()
        return carry

    lax.fori_loop(1, rows, drain, 0)
    for g in range(2):
        def z_drain(zz, carry):
            src = zz * plane + q

            @pl.when((zz <= z) & can_up)
            def _():
                send(g, UP, src).wait_send()

            @pl.when((zz >= z) & can_down)
            def _():
                send(g, DOWN, src).wait_send()

            send(g, FIRST, src).wait_send()
            send(g, SECOND, src).wait_send()
            send(g, SECOND, zz * plane + q1).wait_send()
            return carry

        lax.fori_loop(0, depth, z_drain, 0)

        def m_drain(o, carry):
            send(g, MATE, (row + o) % rows).wait_send()
            return carry

        lax.fori_loop(1, rows, m_drain, 0)


def body(x, ratios, w, retention, credit, gain, scale, offset):
    tile_rows, tile_cols, width = x.shape
    heads = retention.shape[0]
    count = tile_rows * tile_cols
    hd = width // heads
    rows, cols = lax.axis_size("row"), lax.axis_size("col")
    unit = heads * hd // rows
    pairs = heads // 2
    lanes = 2 * hd
    dma = pltpu.SemaphoreType.DMA
    return pl.pallas_call(
        functools.partial(kernel, rows, cols, tile_rows, tile_cols, heads),
        out_shape=jax.ShapeDtypeStruct((tile_rows // 2, tile_cols // 2, 4 * width), BF16),
        in_specs=[pl.BlockSpec(memory_space=pltpu.VMEM)] * 8,
        out_specs=pl.BlockSpec(memory_space=pltpu.VMEM),
        scratch_shapes=[
            pltpu.VMEM((3, 2, width, width // 2), BF16),
            pltpu.VMEM((3, count, width), BF16),
            pltpu.VMEM((3, count, width), BF16),
            pltpu.VMEM((heads, count, count), F32),
            pltpu.VMEM((2, count, width // 4), BF16),
            pltpu.VMEM((2, tile_cols, width // 4), BF16),
            pltpu.VMEM((3, count, heads), F32),
            pltpu.VMEM((8, 128), F32),
            pltpu.VMEM((rows, 8, 128), F32),
            pltpu.VMEM((rows, unit, lanes), BF16),
            pltpu.VMEM((rows, unit, lanes), BF16),
            pltpu.VMEM((rows, unit, lanes), F32),
            pltpu.VMEM((rows, unit, lanes), BF16),
            pltpu.VMEM((rows, unit, lanes), BF16),
            pltpu.VMEM((pairs, count, lanes), F32),
            pltpu.VMEM((2, count, lanes), F32),
            dma((2, 5, rows)),
            dma((2, 2, rows)),
            dma((4,)),
            dma((4,)),
            dma((rows,)),
            dma((rows,)),
            dma((rows,)),
            dma((rows,)),
            dma((rows,)),
            dma((rows,)),
        ],
        compiler_params=pltpu.CompilerParams(
            collective_id=0, has_side_effects=True, vmem_limit_bytes=60 * 1024 * 1024),
    )(
        x.reshape(count, width), ratios, w, retention.reshape(heads, count),
        credit.reshape(1, width), gain.reshape(1, width),
        scale.reshape(1, 4 * width), offset.reshape(1, 4 * width),
    )


def solution(mesh):
    return jax.shard_map(
        body,
        mesh=mesh,
        in_specs=(
            P("row", "col", None),
            P(),
            P(None, "row", None),
            P(None, "row", "col"),
            P(),
            P(),
            P(),
            P(),
        ),
        out_specs=P("row", "col", None),
        check_vma=False,
    )
```

```python
import functools

import jax
import jax.numpy as jnp
from jax import lax
from jax.experimental import pallas as pl
from jax.experimental.pallas import tpu as pltpu
from jax.sharding import PartitionSpec as P

MESH = pl.DeviceIdType.MESH
F32 = jnp.float32
BF16 = jnp.bfloat16
HIGH = lax.Precision.HIGHEST
UP, DOWN, FIRST, SECOND, MATE = range(5)


def iota(shape, dim):
    return lax.broadcasted_iota(jnp.int32, shape, dim)


def kernel(
    rows, cols, tile_rows, tile_cols, heads,
    x_ref, ratio_ref, w_ref, ret_ref, credit_ref, gain_ref, scale_ref, offset_ref,
    out_ref,
    wf, mx, proj, decay, halo_side, halo_row, run_c, mine, totals, kept_all, states, arrived, scan_f, leaving,
    entering, block, stats,
    w_send, w_recv, halo_send, halo_recv, t_send, t_recv, a_send, a_recv, b_send, b_recv,
):
    count, width = x_ref.shape
    hd = width // heads
    pairs = heads // 2
    lanes = 2 * hd
    quarter = width // 4
    share = w_ref.shape[1]
    half_w = width // 2
    unit = states.shape[1]
    row, col = lax.axis_index("row"), lax.axis_index("col")
    plane = 4
    depth = rows // plane
    z, q = row // plane, row % plane
    bx, by = q % 2, q // 2
    half = col % 2
    mate = col + 1 - 2 * half
    q1 = (1 - half) * (q + 1 - 2 * bx) + half * (q + 2 - 4 * by)
    q2 = half * (q + 1 - 2 * bx) + (1 - half) * (q + 2 - 4 * by)
    q12 = plane - 1 - q

    barrier = pltpu.get_barrier_semaphore()
    right, left = (col + 1) % cols, (col + cols - 1) % cols
    down_row, up_row = (row + 1) % rows, (row + rows - 1) % rows
    can_up, can_down = z < depth - 1, z > 0
    has_next, has_previous = row < rows - 1, row > 0

    def greet(target):
        pl.semaphore_signal(barrier, inc=1, device_id=target, device_id_type=MESH)

    greet({"row": z * plane + q1})
    greet({"row": z * plane + q2})
    for other in (right, left, mate):
        greet({"col": other})
    for there, target in (
        (can_up, (row + plane) % rows), (can_down, (row + rows - plane) % rows),
        (has_next, down_row), (has_previous, up_row),
    ):
        @pl.when(there)
        def _():
            greet({"row": target})

    expected = (
        5 + can_up.astype(jnp.int32) + can_down.astype(jnp.int32)
        + has_next.astype(jnp.int32) + has_previous.astype(jnp.int32)
    )
    pl.semaphore_wait(barrier, expected)

    halos = [
        pltpu.make_async_remote_copy(
            x_ref.at[:, 0:quarter], halo_side.at[0], halo_send.at[0], halo_recv.at[0],
            device_id={"col": right}, device_id_type=MESH),
        pltpu.make_async_remote_copy(
            x_ref.at[:, quarter:2 * quarter], halo_side.at[1], halo_send.at[1], halo_recv.at[1],
            device_id={"col": left}, device_id_type=MESH),
        pltpu.make_async_remote_copy(
            x_ref.at[count - tile_cols:count, 2 * quarter:3 * quarter], halo_row.at[0],
            halo_send.at[2], halo_recv.at[2], device_id={"row": down_row}, device_id_type=MESH),
        pltpu.make_async_remote_copy(
            x_ref.at[0:tile_cols, 3 * quarter:], halo_row.at[1],
            halo_send.at[3], halo_recv.at[3], device_id={"row": up_row}, device_id_type=MESH),
    ]

    def sl(g):
        return (g + 1) % 3

    def place(g, side, src):
        return wf.at[sl(g), side, pl.ds(pl.multiple_of(src * share, share), share), :]

    targets = {
        UP: {"row": (row + plane) % rows},
        DOWN: {"row": (row + rows - plane) % rows},
        FIRST: {"row": z * plane + q1},
        SECOND: {"row": z * plane + q2},
        MATE: {"col": mate},
    }

    def send(g, kind, src, own=False):
        source = place(g, half, src)
        if own:
            source = w_ref.at[sl(g), :, pl.ds(pl.multiple_of(half * half_w, half_w), half_w)]
        return pltpu.make_async_remote_copy(
            source, place(g, half, src), w_send.at[g, kind, src], w_recv.at[g, half, src],
            device_id=targets[kind], device_id_type=MESH)

    def got(g, side, src):
        ref = place(g, side, src)
        pltpu.make_async_remote_copy(
            ref, ref, w_send.at[g, MATE, src], w_recv.at[g, side, src],
            device_id=targets[MATE], device_id_type=MESH).wait_recv()

    def own_step(g):
        @pl.when(can_up)
        def _():
            send(g, UP, row, True).start()

        @pl.when(can_down)
        def _():
            send(g, DOWN, row, True).start()

        send(g, SECOND, row, True).start()
        send(g, FIRST, row, True).start()

    def both(d, act):
        if d == 0:
            act(z, None)
            return

        @pl.when(z >= d)
        def _():
            act(z - d, UP)

        @pl.when(z + d < depth)
        def _():
            act(z + d, DOWN)

    def z_step(g, d):
        def act(zz, onward):
            src = zz * plane + q
            got(g, half, src)

            @pl.when(can_up if onward == UP else can_down)
            def _():
                send(g, onward, src).start()

            for kind in (SECOND, FIRST, MATE):
                send(g, kind, src).start()

        both(d, act)

    def first_step(g, d):
        def act(zz, onward):
            src = zz * plane + q1
            got(g, half, src)
            send(g, SECOND, src).start()
            send(g, MATE, src).start()

        both(d, act)

    def second_step(g, d):
        def act(zz, onward):
            for qq in (q2, q12):
                src = zz * plane + qq
                got(g, half, src)
                send(g, MATE, src).start()

        both(d, act)

    def mate_wait(g):
        def one(o, carry):
            got(g, 1 - half, (row + o) % rows)
            return carry

        lax.fori_loop(1, rows, one, 0)

    own_step(0)
    own_step(1)
    halos[0].start()
    halos[1].start()

    @pl.when(has_next)
    def _():
        halos[2].start()

    @pl.when(has_previous)
    def _():
        halos[3].start()

    own_step(2)

    at = pl.ds(pl.multiple_of(row * share, share), share)
    for p in range(3):
        for side in range(2):
            wf[p, side, at, :] = w_ref[p, :, side * half_w:(side + 1) * half_w]

    ret = ret_ref[...]
    tri = (iota((count, count), 0) >= iota((count, count), 1)).astype(F32)
    running_c = lax.dot_general(tri, ret, (((1,), (1,)), ((), ())), precision=HIGH, preferred_element_type=F32)
    running_r = lax.dot_general(ret, tri, (((1,), (1,)), ((), ())), precision=HIGH, preferred_element_type=F32)
    eye = (iota((count, count), 0) == iota((count, count), 1)).astype(F32)
    ret_c = lax.dot_general(eye, ret, (((1,), (1,)), ((), ())), precision=HIGH, preferred_element_type=F32)
    before_c = running_c - ret_c
    before_r = running_r - ret
    total_r = running_c[count - 1:count, :]
    run_c[0] = running_c
    run_c[1] = before_c
    run_c[2] = total_r - running_c
    mine[...] = jnp.broadcast_to(
        jnp.concatenate([total_r, jnp.zeros((1, 128 - heads), F32)], axis=1), (8, 128))
    totals[row] = mine[...]

    def picked(table, h):
        return jnp.sum(jnp.where(iota(table.shape, 1) == h, table, 0.0), axis=1, keepdims=True)

    def picked_row(table, h):
        return jnp.sum(jnp.where(iota(table.shape, 0) == h, table, 0.0), axis=0, keepdims=True)

    def total_copy(o):
        to = (row + o) % rows
        return pltpu.make_async_remote_copy(
            mine, totals.at[row], t_send.at[to], t_recv.at[row],
            device_id={"row": to}, device_id_type=MESH)

    def total_send(o, carry):
        total_copy(o).start()
        return carry

    def z_steps(groups, d):
        if d < depth:
            for g in groups:
                z_step(g, d)

    def first_steps(groups, d):
        if d < depth:
            for g in groups:
                first_step(g, d)

    def second_steps(groups, d):
        if d < depth:
            for g in groups:
                second_step(g, d)

    early = (0, 1)
    z_steps(early, 1)
    first_steps(early, 0)
    second_steps(early, 0)

    halos[0].wait()
    halos[1].wait()

    @pl.when(has_next)
    def _():
        halos[2].wait_send()
        halos[3].wait_recv()

    @pl.when(has_previous)
    def _():
        halos[3].wait_send()
        halos[2].wait_recv()

    token = iota((count, quarter), 0)
    place_in_row = token % tile_cols
    x0 = x_ref[:, 0:quarter].astype(F32)
    x1 = x_ref[:, quarter:2 * quarter].astype(F32)
    side0 = jnp.where(col > 0, halo_side[0].astype(F32), 0.0)
    side1 = jnp.where(col < cols - 1, halo_side[1].astype(F32), 0.0)
    top = jnp.where(row > 0, halo_row[0].astype(F32), 0.0)
    bottom = jnp.where(row < rows - 1, halo_row[1].astype(F32), 0.0)
    last = tile_cols - 1
    shifted = [
        jnp.where(place_in_row == 0, pltpu.roll(side0, count - last, 0), pltpu.roll(x0, 1, 0)),
        jnp.where(place_in_row == last, pltpu.roll(side1, last, 0), pltpu.roll(x1, count - 1, 0)),
        jnp.concatenate([top, x_ref[0:count - tile_cols, 2 * quarter:3 * quarter].astype(F32)], axis=0),
        jnp.concatenate([x_ref[tile_cols:count, 3 * quarter:].astype(F32), bottom], axis=0),
    ]
    for part in range(4):
        span = slice(part * quarter, (part + 1) * quarter)
        xs = x_ref[:, span].astype(F32)
        for p in range(3):
            c = ratio_ref[p:p + 1, span]
            mx[p, :, span] = (xs * c + shifted[part] * (1.0 - c)).astype(BF16)

    earlier = iota((count, count), 0) > iota((count, count), 1)
    diagonal = iota((count, count), 0) == iota((count, count), 1)

    def decays(h, carry):
        rc, bc = picked(run_c[0], h), picked(run_c[1], h)
        rr, br = picked_row(running_r, h), picked_row(before_r, h)
        exponent = jnp.where(earlier, bc - rr, br - rc)
        decay[h] = jnp.where(diagonal, 0.0, jnp.exp(exponent))
        return carry

    for d in range(2, depth):
        z_steps(early, d)
        first_steps(early, d - 1)
        second_steps(early, d - 1)
        if d == 2:
            lax.fori_loop(0, heads // 2, decays, 0)
    z_steps((2,), 1)
    first_steps(early, depth - 1)
    first_steps((2,), 0)
    lax.fori_loop(heads // 2 if depth > 2 else 0, heads, decays, 0)
    second_steps(early, depth - 1)

    def project(p):
        for side in range(2):
            def chunk(i, carry):
                src = pl.ds(pl.multiple_of(i * 256, 256), 256)
                dst = pl.ds(pl.multiple_of(side * half_w + i * 256, 256), 256)
                proj[p, :, dst] = jnp.dot(
                    mx[p], wf[p, side, :, src], preferred_element_type=F32).astype(BF16)
                return carry

            lax.fori_loop(0, half_w // 256, chunk, 0)

    mate_wait(0)
    project(1)
    z_steps((2,), 2)
    first_steps((2,), 1)
    mate_wait(1)
    project(2)
    for d in range(3, depth):
        z_steps((2,), d)
        first_steps((2,), d - 1)

    lane = iota((count, lanes), 1)
    low = lane < hd

    def pair_col(table, i):
        return jnp.where(low, picked(table, 2 * i), picked(table, 2 * i + 1))

    low_u = iota((hd, lanes), 1) < hd
    flat = rows * unit

    def local_states(i, carry):
        span = pl.ds(pl.multiple_of(i * lanes, lanes), lanes)
        k = proj[1, :, span].astype(F32)
        v = proj[2, :, span]
        kd = jnp.concatenate(
            [k * jnp.exp(pair_col(run_c[2], i)), k * jnp.exp(pair_col(run_c[1], i))], axis=1).astype(BF16)
        m = lax.dot_general(kd, v, (((0,), (0,)), ((), ())), preferred_element_type=F32)
        a = jnp.where(low_u, m[0:hd], pltpu.roll(m[2 * hd:3 * hd], hd, 1)).astype(BF16)
        b = jnp.where(low_u, pltpu.roll(m[hd:2 * hd], hd, 1), m[3 * hd:]).astype(BF16)
        per = hd // unit
        for s in range(per):
            states[2 * i * per + s] = a[s * unit:(s + 1) * unit]
            states[(2 * i + 1) * per + s] = b[s * unit:(s + 1) * unit]
        return carry

    lax.fori_loop(0, pairs, local_states, 0)

    def a_copy(o):
        to = (row + o) % rows
        return pltpu.make_async_remote_copy(
            states.at[to], arrived.at[row], a_send.at[to], a_recv.at[row],
            device_id={"row": to}, device_id_type=MESH)

    def a_start(o, carry):
        a_copy(o).start()
        return carry

    lax.fori_loop(1, rows, total_send, 0)
    lax.fori_loop(1, rows, a_start, 0)
    arrived[row] = states[row]

    if depth > 1:
        first_steps((2,), depth - 1)
    for d in range(depth - 1):
        second_steps((2,), d)

    def from_all(dst, send_sem, recv_sem):
        def one(o, carry):
            src = (row + o) % rows
            pltpu.make_async_remote_copy(
                dst.at[src], dst.at[src], send_sem.at[src], recv_sem.at[src],
                device_id={"row": src}, device_id_type=MESH).wait_recv()
            return carry

        lax.fori_loop(1, rows, one, 0)

    from_all(totals, t_send, t_recv)
    from_all(arrived, a_send, a_recv)
    head = (row * unit) // hd

    everyone = totals[...]
    here = iota(everyone.shape, 2) == head
    kept_all[...] = jnp.broadcast_to(
        jnp.exp(jnp.sum(jnp.where(here, everyone, 0.0), axis=2, keepdims=True)), everyone.shape)

    def kept(j):
        return kept_all[j][0:1, :]

    def forward(j, acc):
        scan_f[j] = acc
        return kept(j) * acc + arrived[j].astype(F32)

    def backward(o, acc):
        j = rows - 1 - o
        leaving[j] = jnp.where(iota((unit, lanes), 1) < hd, scan_f[j], acc).astype(BF16)
        return kept(j) * acc + arrived[j].astype(F32)

    lax.fori_loop(0, rows, forward, jnp.zeros((unit, lanes), F32))
    lax.fori_loop(0, rows, backward, jnp.zeros((unit, lanes), F32))

    def b_copy(o):
        to = (row + o) % rows
        return pltpu.make_async_remote_copy(
            leaving.at[to], entering.at[row], b_send.at[to], b_recv.at[row],
            device_id={"row": to}, device_id_type=MESH)

    def b_start(o, carry):
        b_copy(o).start()
        return carry

    lax.fori_loop(1, rows, b_start, 0)
    entering[row] = leaving[row]

    if depth > 1:
        second_steps((2,), depth - 1)
    mate_wait(2)
    project(0)

    def halves(value):
        a = jnp.sum(jnp.where(low, value, 0.0), axis=1, keepdims=True)
        b = jnp.sum(jnp.where(low, 0.0, value), axis=1, keepdims=True)
        return jnp.where(low, a, b)

    def local_mix(i, carry):
        span = pl.ds(pl.multiple_of(i * lanes, lanes), lanes)
        r, k, v = proj[0, :, span], proj[1, :, span], proj[2, :, span]
        outs = []
        for s in range(2):
            rs = jnp.where(low if s == 0 else jnp.logical_not(low), r.astype(F32), 0.0).astype(BF16)
            scores = lax.dot_general(rs, k, (((1,), (1,)), ((), ())), preferred_element_type=F32)
            weight = (scores * decay[2 * i + s]).astype(BF16)
            outs.append(jnp.dot(weight, v, preferred_element_type=F32))
        own = halves(r.astype(F32) * credit_ref[:, span] * k.astype(F32)) * v.astype(F32)
        block[i] = jnp.where(low, outs[0], outs[1]) + own
        return carry

    lax.fori_loop(0, pairs, local_mix, 0)
    from_all(entering, b_send, b_recv)

    def finish(i, total):
        span = pl.ds(pl.multiple_of(i * lanes, lanes), lanes)
        r = proj[0, :, span]
        per = hd // unit
        a = jnp.concatenate([entering[2 * i * per + s].astype(F32) for s in range(per)], axis=0)
        b = jnp.concatenate([entering[(2 * i + 1) * per + s].astype(F32) for s in range(per)], axis=0)
        fwd = jnp.concatenate(
            [jnp.where(low_u, a, 0.0), jnp.where(low_u, 0.0, pltpu.roll(b, hd, 1))], axis=0).astype(BF16)
        bwd = jnp.concatenate(
            [jnp.where(low_u, pltpu.roll(a, hd, 1), 0.0), jnp.where(low_u, 0.0, b)], axis=0).astype(BF16)
        wkv = (
            block[i]
            + jnp.exp(pair_col(run_c[1], i)) * jnp.dot(r, fwd, preferred_element_type=F32)
            + jnp.exp(pair_col(run_c[2], i)) * jnp.dot(r, bwd, preferred_element_type=F32)
        )
        centred = wkv - halves(wkv) * (1.0 / hd)
        variance = halves(centred * centred) * (1.0 / hd)
        made = x_ref[:, span].astype(F32) + centred * lax.rsqrt(variance + 1e-05) * gain_ref[:, span]
        block[i] = made
        return total + made

    total = lax.fori_loop(0, pairs, finish, jnp.zeros((count, lanes), F32))
    group = (
        (iota((count, count), 0) // (2 * tile_cols) == iota((count, count), 1) // (2 * tile_cols))
        & (iota((count, count), 0) % tile_cols // 2 == iota((count, count), 1) % tile_cols // 2)
    ).astype(F32)

    def over_group(value):
        rowsum = jnp.broadcast_to(jnp.sum(value, axis=1, keepdims=True), (count, lanes))
        return jnp.dot(group, rowsum, precision=HIGH, preferred_element_type=F32) * (1.0 / (4 * width))

    mean = over_group(total)

    def spread(i, acc):
        dev = block[i] - mean
        return acc + dev * dev

    variance = over_group(lax.fori_loop(0, pairs, spread, jnp.zeros((count, lanes), F32)))
    stats[0] = mean
    stats[1] = lax.rsqrt(variance + 1e-05)
    half_cols = tile_cols // 2

    def emit(i, carry):
        for part in range(4):
            span = pl.ds(pl.multiple_of(part * width + i * lanes, lanes), lanes)
            g, o = scale_ref[:, span], offset_ref[:, span]
            for a in range(tile_rows // 2):
                take = pl.ds((2 * a + part % 2) * tile_cols + part // 2, half_cols, stride=2)
                value = (block[i, take, :] - stats[0, take, :]) * stats[1, take, :]
                out_ref[a, :, span] = (value * g + o).astype(BF16)
        return carry

    lax.fori_loop(0, pairs, emit, 0)

    def drain(o, carry):
        total_copy(o).wait_send()
        a_copy(o).wait_send()
        b_copy(o).wait_send()
        return carry

    lax.fori_loop(1, rows, drain, 0)
    for g in range(3):
        def z_drain(zz, carry):
            src = zz * plane + q

            @pl.when((zz <= z) & can_up)
            def _():
                send(g, UP, src).wait_send()

            @pl.when((zz >= z) & can_down)
            def _():
                send(g, DOWN, src).wait_send()

            send(g, FIRST, src).wait_send()
            send(g, SECOND, src).wait_send()
            send(g, SECOND, zz * plane + q1).wait_send()
            return carry

        lax.fori_loop(0, depth, z_drain, 0)

        def m_drain(o, carry):
            send(g, MATE, (row + o) % rows).wait_send()
            return carry

        lax.fori_loop(1, rows, m_drain, 0)


def body(x, ratios, w, retention, credit, gain, scale, offset):
    tile_rows, tile_cols, width = x.shape
    heads = retention.shape[0]
    count = tile_rows * tile_cols
    hd = width // heads
    rows, cols = lax.axis_size("row"), lax.axis_size("col")
    unit = heads * hd // rows
    pairs = heads // 2
    lanes = 2 * hd
    dma = pltpu.SemaphoreType.DMA
    return pl.pallas_call(
        functools.partial(kernel, rows, cols, tile_rows, tile_cols, heads),
        out_shape=jax.ShapeDtypeStruct((tile_rows // 2, tile_cols // 2, 4 * width), BF16),
        in_specs=[pl.BlockSpec(memory_space=pltpu.VMEM)] * 8,
        out_specs=pl.BlockSpec(memory_space=pltpu.VMEM),
        scratch_shapes=[
            pltpu.VMEM((3, 2, width, width // 2), BF16),
            pltpu.VMEM((3, count, width), BF16),
            pltpu.VMEM((3, count, width), BF16),
            pltpu.VMEM((heads, count, count), F32),
            pltpu.VMEM((2, count, width // 4), BF16),
            pltpu.VMEM((2, tile_cols, width // 4), BF16),
            pltpu.VMEM((3, count, heads), F32),
            pltpu.VMEM((8, 128), F32),
            pltpu.VMEM((rows, 8, 128), F32),
            pltpu.VMEM((rows, 8, 128), F32),
            pltpu.VMEM((rows, unit, lanes), BF16),
            pltpu.VMEM((rows, unit, lanes), BF16),
            pltpu.VMEM((rows, unit, lanes), F32),
            pltpu.VMEM((rows, unit, lanes), BF16),
            pltpu.VMEM((rows, unit, lanes), BF16),
            pltpu.VMEM((pairs, count, lanes), F32),
            pltpu.VMEM((2, count, lanes), F32),
            dma((3, 5, rows)),
            dma((3, 2, rows)),
            dma((4,)),
            dma((4,)),
            dma((rows,)),
            dma((rows,)),
            dma((rows,)),
            dma((rows,)),
            dma((rows,)),
            dma((rows,)),
        ],
        compiler_params=pltpu.CompilerParams(
            collective_id=0, has_side_effects=True, vmem_limit_bytes=60 * 1024 * 1024),
    )(
        x.reshape(count, width), ratios, w, retention.reshape(heads, count),
        credit.reshape(1, width), gain.reshape(1, width),
        scale.reshape(1, 4 * width), offset.reshape(1, 4 * width),
    )


def solution(mesh):
    return jax.shard_map(
        body,
        mesh=mesh,
        in_specs=(
            P("row", "col", None),
            P(),
            P(None, "row", None),
            P(None, "row", "col"),
            P(),
            P(),
            P(),
            P(),
        ),
        out_specs=P("row", "col", None),
        check_vma=False,
    )
```

```python
import functools

import jax
import jax.numpy as jnp
from jax import lax
from jax.experimental import pallas as pl
from jax.experimental.pallas import tpu as pltpu
from jax.sharding import PartitionSpec as P

MESH = pl.DeviceIdType.MESH
F32 = jnp.float32
BF16 = jnp.bfloat16
HIGH = lax.Precision.HIGHEST
UP, DOWN, FIRST, SECOND, MATE = range(5)


def iota(shape, dim):
    return lax.broadcasted_iota(jnp.int32, shape, dim)


def kernel(
    rows, cols, tile_rows, tile_cols, heads,
    x_ref, ratio_ref, w_ref, ret_ref, credit_ref, gain_ref, scale_ref, offset_ref,
    out_ref,
    wf, mx, proj, decay, halo_side, halo_row, run_c, mine, totals, kept_all, states, arrived, scan_f, leaving,
    entering, block, stats,
    w_send, w_recv, halo_send, halo_recv, t_send, t_recv, a_send, a_recv, b_send, b_recv,
):
    count, width = x_ref.shape
    hd = width // heads
    pairs = heads // 2
    lanes = 2 * hd
    quarter = width // 4
    share = w_ref.shape[1]
    half_w = width // 2
    unit = states.shape[1]
    row, col = lax.axis_index("row"), lax.axis_index("col")
    plane = 4
    depth = rows // plane
    z, q = row // plane, row % plane
    bx, by = q % 2, q // 2
    half = col % 2
    mate = col + 1 - 2 * half
    q1 = (1 - half) * (q + 1 - 2 * bx) + half * (q + 2 - 4 * by)
    q2 = half * (q + 1 - 2 * bx) + (1 - half) * (q + 2 - 4 * by)
    q12 = plane - 1 - q

    barrier = pltpu.get_barrier_semaphore()
    right, left = (col + 1) % cols, (col + cols - 1) % cols
    down_row, up_row = (row + 1) % rows, (row + rows - 1) % rows
    can_up, can_down = z < depth - 1, z > 0
    has_next, has_previous = row < rows - 1, row > 0

    def greet(target):
        pl.semaphore_signal(barrier, inc=1, device_id=target, device_id_type=MESH)

    greet({"row": z * plane + q1})
    greet({"row": z * plane + q2})
    for other in (right, left, mate):
        greet({"col": other})
    for there, target in (
        (can_up, (row + plane) % rows), (can_down, (row + rows - plane) % rows),
        (has_next, down_row), (has_previous, up_row),
    ):
        @pl.when(there)
        def _():
            greet({"row": target})

    expected = (
        5 + can_up.astype(jnp.int32) + can_down.astype(jnp.int32)
        + has_next.astype(jnp.int32) + has_previous.astype(jnp.int32)
    )
    pl.semaphore_wait(barrier, expected)

    halos = [
        pltpu.make_async_remote_copy(
            x_ref.at[:, 0:quarter], halo_side.at[0], halo_send.at[0], halo_recv.at[0],
            device_id={"col": right}, device_id_type=MESH),
        pltpu.make_async_remote_copy(
            x_ref.at[:, quarter:2 * quarter], halo_side.at[1], halo_send.at[1], halo_recv.at[1],
            device_id={"col": left}, device_id_type=MESH),
        pltpu.make_async_remote_copy(
            x_ref.at[count - tile_cols:count, 2 * quarter:3 * quarter], halo_row.at[0],
            halo_send.at[2], halo_recv.at[2], device_id={"row": down_row}, device_id_type=MESH),
        pltpu.make_async_remote_copy(
            x_ref.at[0:tile_cols, 3 * quarter:], halo_row.at[1],
            halo_send.at[3], halo_recv.at[3], device_id={"row": up_row}, device_id_type=MESH),
    ]

    def sl(g):
        return (g + 1) % 3

    def place(g, side, src):
        return wf.at[sl(g), side, pl.ds(pl.multiple_of(src * share, share), share), :]

    targets = {
        UP: {"row": (row + plane) % rows},
        DOWN: {"row": (row + rows - plane) % rows},
        FIRST: {"row": z * plane + q1},
        SECOND: {"row": z * plane + q2},
        MATE: {"col": mate},
    }

    def send(g, kind, src, own=False):
        source = place(g, half, src)
        if own:
            source = w_ref.at[sl(g), :, pl.ds(pl.multiple_of(half * half_w, half_w), half_w)]
        return pltpu.make_async_remote_copy(
            source, place(g, half, src), w_send.at[g, kind, src], w_recv.at[g, half, src],
            device_id=targets[kind], device_id_type=MESH)

    def got(g, side, src):
        ref = place(g, side, src)
        pltpu.make_async_remote_copy(
            ref, ref, w_send.at[g, MATE, src], w_recv.at[g, side, src],
            device_id=targets[MATE], device_id_type=MESH).wait_recv()

    def own_step(g):
        @pl.when(can_up)
        def _():
            send(g, UP, row, True).start()

        @pl.when(can_down)
        def _():
            send(g, DOWN, row, True).start()

        send(g, SECOND, row, True).start()
        send(g, FIRST, row, True).start()

    def both(d, act):
        if d == 0:
            act(z, None)
            return

        @pl.when(z >= d)
        def _():
            act(z - d, UP)

        @pl.when(z + d < depth)
        def _():
            act(z + d, DOWN)

    def z_step(g, d):
        def act(zz, onward):
            src = zz * plane + q
            got(g, half, src)

            @pl.when(can_up if onward == UP else can_down)
            def _():
                send(g, onward, src).start()

            for kind in (SECOND, FIRST, MATE):
                send(g, kind, src).start()

        both(d, act)

    def first_step(g, d):
        def act(zz, onward):
            src = zz * plane + q1
            got(g, half, src)
            send(g, SECOND, src).start()
            send(g, MATE, src).start()

        both(d, act)

    def second_step(g, d):
        def act(zz, onward):
            for qq in (q2, q12):
                src = zz * plane + qq
                got(g, half, src)
                send(g, MATE, src).start()

        both(d, act)

    def mate_wait(g):
        def one(o, carry):
            got(g, 1 - half, (row + o) % rows)
            return carry

        lax.fori_loop(1, rows, one, 0)

    own_step(0)
    own_step(1)
    halos[0].start()
    halos[1].start()

    @pl.when(has_next)
    def _():
        halos[2].start()

    @pl.when(has_previous)
    def _():
        halos[3].start()

    own_step(2)

    at = pl.ds(pl.multiple_of(row * share, share), share)
    for p in range(3):
        for side in range(2):
            wf[p, side, at, :] = w_ref[p, :, side * half_w:(side + 1) * half_w]

    ret = jnp.concatenate([ret_ref[:, r, :] for r in range(tile_rows)], axis=1)
    tri = (iota((count, count), 0) >= iota((count, count), 1)).astype(F32)
    running_c = lax.dot_general(tri, ret, (((1,), (1,)), ((), ())), precision=HIGH, preferred_element_type=F32)
    running_r = lax.dot_general(ret, tri, (((1,), (1,)), ((), ())), precision=HIGH, preferred_element_type=F32)
    eye = (iota((count, count), 0) == iota((count, count), 1)).astype(F32)
    ret_c = lax.dot_general(eye, ret, (((1,), (1,)), ((), ())), precision=HIGH, preferred_element_type=F32)
    before_c = running_c - ret_c
    before_r = running_r - ret
    total_r = running_c[count - 1:count, :]
    run_c[0] = running_c
    run_c[1] = before_c
    run_c[2] = total_r - running_c
    mine[...] = jnp.broadcast_to(
        jnp.concatenate([total_r, jnp.zeros((1, 128 - heads), F32)], axis=1), (8, 128))
    totals[row] = mine[...]

    def picked(table, h):
        return jnp.sum(jnp.where(iota(table.shape, 1) == h, table, 0.0), axis=1, keepdims=True)

    def picked_row(table, h):
        return jnp.sum(jnp.where(iota(table.shape, 0) == h, table, 0.0), axis=0, keepdims=True)

    def total_copy(o):
        to = (row + o) % rows
        return pltpu.make_async_remote_copy(
            mine, totals.at[row], t_send.at[to], t_recv.at[row],
            device_id={"row": to}, device_id_type=MESH)

    def total_send(o, carry):
        total_copy(o).start()
        return carry

    issued = set()

    def once(step, g, d):
        if d < depth and (step, g, d) not in issued:
            issued.add((step, g, d))
            step(g, d)

    def z_steps(groups, d):
        for g in groups:
            once(z_step, g, d)

    def first_steps(groups, d):
        for g in groups:
            once(first_step, g, d)

    def second_steps(groups, d):
        for g in groups:
            once(second_step, g, d)

    early = (0, 1)
    z_steps(early, 1)
    first_steps(early, 0)
    z_steps(early, 2)
    first_steps(early, 1)

    halos[0].wait()
    halos[1].wait()

    @pl.when(has_next)
    def _():
        halos[2].wait_send()
        halos[3].wait_recv()

    @pl.when(has_previous)
    def _():
        halos[3].wait_send()
        halos[2].wait_recv()

    token = iota((count, quarter), 0)
    place_in_row = token % tile_cols
    x0 = x_ref[:, 0:quarter].astype(F32)
    x1 = x_ref[:, quarter:2 * quarter].astype(F32)
    side0 = jnp.where(col > 0, halo_side[0].astype(F32), 0.0)
    side1 = jnp.where(col < cols - 1, halo_side[1].astype(F32), 0.0)
    top = jnp.where(row > 0, halo_row[0].astype(F32), 0.0)
    bottom = jnp.where(row < rows - 1, halo_row[1].astype(F32), 0.0)
    last = tile_cols - 1
    shifted = [
        jnp.where(place_in_row == 0, pltpu.roll(side0, count - last, 0), pltpu.roll(x0, 1, 0)),
        jnp.where(place_in_row == last, pltpu.roll(side1, last, 0), pltpu.roll(x1, count - 1, 0)),
        jnp.concatenate([top, x_ref[0:count - tile_cols, 2 * quarter:3 * quarter].astype(F32)], axis=0),
        jnp.concatenate([x_ref[tile_cols:count, 3 * quarter:].astype(F32), bottom], axis=0),
    ]
    for part in range(4):
        span = slice(part * quarter, (part + 1) * quarter)
        xs = x_ref[:, span].astype(F32)
        for p in range(3):
            c = ratio_ref[p:p + 1, span]
            mx[p, :, span] = (xs * c + shifted[part] * (1.0 - c)).astype(BF16)

    earlier = iota((count, count), 0) > iota((count, count), 1)
    diagonal = iota((count, count), 0) == iota((count, count), 1)

    def decays(h, carry):
        rc, bc = picked(run_c[0], h), picked(run_c[1], h)
        rr, br = picked_row(running_r, h), picked_row(before_r, h)
        exponent = jnp.where(earlier, bc - rr, br - rc)
        decay[h] = jnp.where(diagonal, 0.0, jnp.exp(exponent))
        return carry

    for d in range(3, depth):
        z_steps(early, d)
        first_steps(early, d - 1)
    z_steps((2,), 1)
    first_steps((2,), 0)
    first_steps(early, depth - 1)
    lax.fori_loop(0, heads // 2, decays, 0)
    z_steps((2,), 2)
    first_steps((2,), 1)
    for d in range(depth - 1):
        second_steps(early, d)
    lax.fori_loop(heads // 2, heads, decays, 0)
    for d in range(3, depth):
        z_steps((2,), d)
        first_steps((2,), d - 1)
    first_steps((2,), depth - 1)
    second_steps(early, depth - 1)

    def project(p):
        for side in range(2):
            def chunk(i, carry):
                src = pl.ds(pl.multiple_of(i * 256, 256), 256)
                dst = pl.ds(pl.multiple_of(side * half_w + i * 256, 256), 256)
                proj[p, :, dst] = jnp.dot(
                    mx[p], wf[p, side, :, src], preferred_element_type=F32).astype(BF16)
                return carry

            lax.fori_loop(0, half_w // 256, chunk, 0)

    mate_wait(0)
    project(1)
    mate_wait(1)
    project(2)

    lane = iota((count, lanes), 1)
    low = lane < hd

    def pair_col(table, i):
        return jnp.where(low, picked(table, 2 * i), picked(table, 2 * i + 1))

    low_u = iota((hd, lanes), 1) < hd
    flat = rows * unit

    def local_states(i, carry):
        span = pl.ds(pl.multiple_of(i * lanes, lanes), lanes)
        k = proj[1, :, span].astype(F32)
        v = proj[2, :, span]
        kd = jnp.concatenate(
            [k * jnp.exp(pair_col(run_c[2], i)), k * jnp.exp(pair_col(run_c[1], i))], axis=1).astype(BF16)
        m = lax.dot_general(kd, v, (((0,), (0,)), ((), ())), preferred_element_type=F32)
        a = jnp.where(low_u, m[0:hd], pltpu.roll(m[2 * hd:3 * hd], hd, 1)).astype(BF16)
        b = jnp.where(low_u, pltpu.roll(m[hd:2 * hd], hd, 1), m[3 * hd:]).astype(BF16)
        per = hd // unit
        for s in range(per):
            states[2 * i * per + s] = a[s * unit:(s + 1) * unit]
            states[(2 * i + 1) * per + s] = b[s * unit:(s + 1) * unit]
        return carry

    lax.fori_loop(0, pairs, local_states, 0)

    def a_copy(o):
        to = (row + o) % rows
        return pltpu.make_async_remote_copy(
            states.at[to], arrived.at[row], a_send.at[to], a_recv.at[row],
            device_id={"row": to}, device_id_type=MESH)

    def a_start(o, carry):
        a_copy(o).start()
        return carry

    lax.fori_loop(1, rows, total_send, 0)
    lax.fori_loop(1, rows, a_start, 0)
    arrived[row] = states[row]

    for d in range(depth - 1):
        second_steps((2,), d)

    def from_all(dst, send_sem, recv_sem):
        def one(o, carry):
            src = (row + o) % rows
            pltpu.make_async_remote_copy(
                dst.at[src], dst.at[src], send_sem.at[src], recv_sem.at[src],
                device_id={"row": src}, device_id_type=MESH).wait_recv()
            return carry

        lax.fori_loop(1, rows, one, 0)

    from_all(totals, t_send, t_recv)
    from_all(arrived, a_send, a_recv)
    head = (row * unit) // hd

    everyone = totals[...]
    here = iota(everyone.shape, 2) == head
    kept_all[...] = jnp.broadcast_to(
        jnp.exp(jnp.sum(jnp.where(here, everyone, 0.0), axis=2, keepdims=True)), everyone.shape)

    def kept(j):
        return kept_all[j][0:1, :]

    def forward(j, acc):
        scan_f[j] = acc
        return kept(j) * acc + arrived[j].astype(F32)

    def backward(o, acc):
        j = rows - 1 - o
        leaving[j] = jnp.where(iota((unit, lanes), 1) < hd, scan_f[j], acc).astype(BF16)
        return kept(j) * acc + arrived[j].astype(F32)

    lax.fori_loop(0, rows, forward, jnp.zeros((unit, lanes), F32))
    lax.fori_loop(0, rows, backward, jnp.zeros((unit, lanes), F32))

    def b_copy(o):
        to = (row + o) % rows
        return pltpu.make_async_remote_copy(
            leaving.at[to], entering.at[row], b_send.at[to], b_recv.at[row],
            device_id={"row": to}, device_id_type=MESH)

    def b_start(o, carry):
        b_copy(o).start()
        return carry

    lax.fori_loop(1, rows, b_start, 0)
    entering[row] = leaving[row]

    second_steps((2,), depth - 1)
    mate_wait(2)
    project(0)

    def halves(value):
        a = jnp.sum(jnp.where(low, value, 0.0), axis=1, keepdims=True)
        b = jnp.sum(jnp.where(low, 0.0, value), axis=1, keepdims=True)
        return jnp.where(low, a, b)

    def local_mix(i, carry):
        span = pl.ds(pl.multiple_of(i * lanes, lanes), lanes)
        r, k, v = proj[0, :, span], proj[1, :, span], proj[2, :, span]
        outs = []
        for s in range(2):
            rs = jnp.where(low if s == 0 else jnp.logical_not(low), r.astype(F32), 0.0).astype(BF16)
            scores = lax.dot_general(rs, k, (((1,), (1,)), ((), ())), preferred_element_type=F32)
            weight = (scores * decay[2 * i + s]).astype(BF16)
            outs.append(jnp.dot(weight, v, preferred_element_type=F32))
        own = halves(r.astype(F32) * credit_ref[:, span] * k.astype(F32)) * v.astype(F32)
        block[i] = jnp.where(low, outs[0], outs[1]) + own
        return carry

    lax.fori_loop(0, pairs, local_mix, 0)
    from_all(entering, b_send, b_recv)

    def finish(i, total):
        span = pl.ds(pl.multiple_of(i * lanes, lanes), lanes)
        r = proj[0, :, span]
        per = hd // unit
        a = jnp.concatenate([entering[2 * i * per + s].astype(F32) for s in range(per)], axis=0)
        b = jnp.concatenate([entering[(2 * i + 1) * per + s].astype(F32) for s in range(per)], axis=0)
        fwd = jnp.concatenate(
            [jnp.where(low_u, a, 0.0), jnp.where(low_u, 0.0, pltpu.roll(b, hd, 1))], axis=0).astype(BF16)
        bwd = jnp.concatenate(
            [jnp.where(low_u, pltpu.roll(a, hd, 1), 0.0), jnp.where(low_u, 0.0, b)], axis=0).astype(BF16)
        wkv = (
            block[i]
            + jnp.exp(pair_col(run_c[1], i)) * jnp.dot(r, fwd, preferred_element_type=F32)
            + jnp.exp(pair_col(run_c[2], i)) * jnp.dot(r, bwd, preferred_element_type=F32)
        )
        centred = wkv - halves(wkv) * (1.0 / hd)
        variance = halves(centred * centred) * (1.0 / hd)
        made = x_ref[:, span].astype(F32) + centred * lax.rsqrt(variance + 1e-05) * gain_ref[:, span]
        block[i] = made
        return total + made

    total = lax.fori_loop(0, pairs, finish, jnp.zeros((count, lanes), F32))
    group = (
        (iota((count, count), 0) // (2 * tile_cols) == iota((count, count), 1) // (2 * tile_cols))
        & (iota((count, count), 0) % tile_cols // 2 == iota((count, count), 1) % tile_cols // 2)
    ).astype(F32)

    def over_group(value):
        rowsum = jnp.broadcast_to(jnp.sum(value, axis=1, keepdims=True), (count, lanes))
        return jnp.dot(group, rowsum, precision=HIGH, preferred_element_type=F32) * (1.0 / (4 * width))

    mean = over_group(total)

    def spread(i, acc):
        dev = block[i] - mean
        return acc + dev * dev

    variance = over_group(lax.fori_loop(0, pairs, spread, jnp.zeros((count, lanes), F32)))
    stats[0] = mean
    stats[1] = lax.rsqrt(variance + 1e-05)
    half_cols = tile_cols // 2

    def emit(i, carry):
        for part in range(4):
            span = pl.ds(pl.multiple_of(part * width + i * lanes, lanes), lanes)
            g, o = scale_ref[:, span], offset_ref[:, span]
            for a in range(tile_rows // 2):
                take = pl.ds((2 * a + part % 2) * tile_cols + part // 2, half_cols, stride=2)
                value = (block[i, take, :] - stats[0, take, :]) * stats[1, take, :]
                out_ref[a, :, span] = (value * g + o).astype(BF16)
        return carry

    lax.fori_loop(0, pairs, emit, 0)

    def drain(o, carry):
        total_copy(o).wait_send()
        a_copy(o).wait_send()
        b_copy(o).wait_send()
        return carry

    lax.fori_loop(1, rows, drain, 0)
    for g in range(3):
        def z_drain(zz, carry):
            src = zz * plane + q

            @pl.when((zz <= z) & can_up)
            def _():
                send(g, UP, src).wait_send()

            @pl.when((zz >= z) & can_down)
            def _():
                send(g, DOWN, src).wait_send()

            send(g, FIRST, src).wait_send()
            send(g, SECOND, src).wait_send()
            send(g, SECOND, zz * plane + q1).wait_send()
            return carry

        lax.fori_loop(0, depth, z_drain, 0)

        def m_drain(o, carry):
            send(g, MATE, (row + o) % rows).wait_send()
            return carry

        lax.fori_loop(1, rows, m_drain, 0)


def body(x, ratios, w, retention, credit, gain, scale, offset):
    tile_rows, tile_cols, width = x.shape
    heads = retention.shape[0]
    count = tile_rows * tile_cols
    hd = width // heads
    rows, cols = lax.axis_size("row"), lax.axis_size("col")
    unit = heads * hd // rows
    pairs = heads // 2
    lanes = 2 * hd
    dma = pltpu.SemaphoreType.DMA
    return pl.pallas_call(
        functools.partial(kernel, rows, cols, tile_rows, tile_cols, heads),
        out_shape=jax.ShapeDtypeStruct((tile_rows // 2, tile_cols // 2, 4 * width), BF16),
        in_specs=[pl.BlockSpec(memory_space=pltpu.VMEM)] * 8,
        out_specs=pl.BlockSpec(memory_space=pltpu.VMEM),
        scratch_shapes=[
            pltpu.VMEM((3, 2, width, width // 2), BF16),
            pltpu.VMEM((3, count, width), BF16),
            pltpu.VMEM((3, count, width), BF16),
            pltpu.VMEM((heads, count, count), F32),
            pltpu.VMEM((2, count, width // 4), BF16),
            pltpu.VMEM((2, tile_cols, width // 4), BF16),
            pltpu.VMEM((3, count, heads), F32),
            pltpu.VMEM((8, 128), F32),
            pltpu.VMEM((rows, 8, 128), F32),
            pltpu.VMEM((rows, 8, 128), F32),
            pltpu.VMEM((rows, unit, lanes), BF16),
            pltpu.VMEM((rows, unit, lanes), BF16),
            pltpu.VMEM((rows, unit, lanes), F32),
            pltpu.VMEM((rows, unit, lanes), BF16),
            pltpu.VMEM((rows, unit, lanes), BF16),
            pltpu.VMEM((pairs, count, lanes), F32),
            pltpu.VMEM((2, count, lanes), F32),
            dma((3, 5, rows)),
            dma((3, 2, rows)),
            dma((4,)),
            dma((4,)),
            dma((rows,)),
            dma((rows,)),
            dma((rows,)),
            dma((rows,)),
            dma((rows,)),
            dma((rows,)),
        ],
        compiler_params=pltpu.CompilerParams(
            collective_id=0, has_side_effects=True, vmem_limit_bytes=60 * 1024 * 1024),
    )(
        x.reshape(count, width), ratios, w, retention,
        credit.reshape(1, width), gain.reshape(1, width),
        scale.reshape(1, 4 * width), offset.reshape(1, 4 * width),
    )


def solution(mesh):
    return jax.shard_map(
        body,
        mesh=mesh,
        in_specs=(
            P("row", "col", None),
            P(),
            P(None, "row", None),
            P(None, "row", "col"),
            P(),
            P(),
            P(),
            P(),
        ),
        out_specs=P("row", "col", None),
        check_vma=False,
    )
```
